32 devices in a mesh: dp: 4 (over x, core), expert: 8 (over z, y).
Axes of the slice: x: 2, y: 2, z: 4, core: 2. Of those that a mesh axis runs over, the one named last changes fastest.
Arguments:
- attended: bfloat16 [4096, 1536], P(('dp', 'expert')), may hold values from -6 to 6
- residual: bfloat16 [4096, 1536], P(('dp', 'expert')), may hold values from -6 to 6
- new_kv: bfloat16 [4096, 1024], P(('dp', 'expert')), may hold values from -6 to 6
- kv_pool: bfloat16 [256, 128, 1024], P(('dp', 'expert')), may hold values from -6 to 6
- page_table: int32 [32], P(('dp', 'expert')), may hold values from 0 to 7, as said below
- out_weight: bfloat16 [1536, 1536], P(('dp', 'expert')), may hold values from -0.3125 to 0.3125
- router: bfloat16 [1536, 40], P(('dp', 'expert')), may hold values from -0.15625 to 0.15625
- attn_gain: bfloat16 [1536], P(('dp', 'expert')), may hold values from 0.099609375 to 1.8984375
- ffn_gain: bfloat16 [1536], P(('dp', 'expert')), may hold values from 0.099609375 to 1.8984375
- routes: int32 [4096, 8], P(('dp', 'expert')), may hold values from 0 to 39, all different within a row
- replica_pick: int32 [4096, 8], P(('dp', 'expert')), may hold values from 0 to 5039
- lengths: int32 [5], replicated, may hold values from 1 to 2048, 4096 in all
- slot_expert: int32 [48], replicated, may hold values from 0 to 39, as said below
- slot_capacity: int32 [48], replicated, may hold values from 16 to 32, as said below
- slot_in: bfloat16 [48, 1536, 1024], P('expert', 'dp'), may hold values from -0.15625 to 0.15625
- slot_out: bfloat16 [48, 1536, 512], P('expert', 'dp'), may hold values from -0.25 to 0.25
Outputs:
- residual_out: bfloat16 [4096, 1536], P(('dp', 'expert'))
- next_normed: bfloat16 [4096, 1536], P(('dp', 'expert'))
- pool_out: bfloat16 [256, 128, 1024], P(('dp', 'expert'))
The draws below stay inside these ranges and needn't reach their ends.
Inputs may be any that keep to these rules, and one draw needn't show every extreme that they name: `page_table`: each device's 1 entries differ from one another. `slot_expert`: every expert is held by one slot or more. `slot_capacity`: some slot accepts exactly 32 rows. The capacities of the 6 slots of one index of expert (slots i * 6 to i * 6 + 5) sum to at most 144, and to exactly 144 for some index.
All inputs are finite; a program needn't handle non-finite values.
Results may differ from the reference program's by a relative error of at most 0.0095.
Values may be sent and summed in bfloat16 or wider, within the bound.
A program may use at most 128 MiB of HBM per device.

```python
import math
import jax
import jax.numpy as jnp
import numpy as np
from jax import lax

D = 1536
FFE = 512
EXPERTS = 40
TOP = 8
PAGE = 128
ROWS_DEV = 128
POOL_DEV = 8
ROWS = 4096
KVW = 1024
PAGES_DEV = 1
PAGES = 32
POOL = 256
SLOTS_DEV = 6
SLOTS = 48
CAP = 32
HOLD = 144
DEVICES = 32


def draw_page_table(key, part):
    device_keys = jax.random.split(key, DEVICES)

    def one_device(device_key):
        return jax.random.permutation(device_key, POOL_DEV)[:PAGES_DEV]
    return jax.vmap(one_device)(device_keys).reshape(PAGES).astype(jnp.int32)


def draw_slot_expert(key, part):
    key_extra, key_order = jax.random.split(key)
    extra = jax.random.randint(key_extra, (SLOTS - EXPERTS,), 0, EXPERTS).astype(jnp.int32)
    listing = jnp.concatenate([jnp.arange(EXPERTS, dtype=jnp.int32), extra])
    return jax.random.permutation(key_order, listing).astype(jnp.int32)


def draw_slot_capacity(key, part):
    key_levels, key_holder, key_shift = jax.random.split(key, 3)
    holders = SLOTS // SLOTS_DEV
    low = CAP // 2
    half = CAP - low
    spare = HOLD - SLOTS_DEV * low
    extras = jax.random.randint(key_levels, (holders, SLOTS_DEV), 0, half + 1).astype(jnp.int32)
    sums = jnp.sum(extras, axis=1, keepdims=True)
    scaled = extras * spare // jnp.maximum(sums, spare)
    column = jnp.arange(SLOTS_DEV, dtype=jnp.int32)
    remain = spare - half
    others = jnp.clip(remain - (column - 1) * half, 0, half)
    fullrow = jnp.where(column == 0, half, others).astype(jnp.int32)
    shift = jax.random.randint(key_shift, (), 0, SLOTS_DEV)
    fullrow = jnp.roll(fullrow, shift)
    chosen = jax.random.randint(key_holder, (), 0, holders)
    scaled = scaled.at[chosen].set(fullrow)
    return (low + scaled).reshape(SLOTS).astype(jnp.int32)


def touch_ends(values, key, least, high):
    dims = values.shape
    index_at = [jax.random.randint(jax.random.fold_in(key, axis), (), 0, dims[axis]) for axis in range(len(dims))]
    values = values.at[tuple(index_at)].set(least)
    longest = dims.index(max(dims))
    index_at[longest] = (index_at[longest] + 1) % dims[longest]
    return values.at[tuple(index_at)].set(high)


def spiked(array, stream_key, source, target, blocks, factor):
    owner, partner = [(jnp.arange(array.shape[dim]) // (array.shape[dim] // blocks)).reshape([-1 if axis == dim else 1 for axis in range(array.ndim)]) for dim in (source, target)]
    chosen = jax.random.permutation(stream_key, blocks)[partner]
    strong = (owner == chosen) | (owner == (partner + blocks // 2) % blocks)
    return jnp.where(strong, factor * array, array)


def block_levels(key, dims, pieces, low, largest):
    def one(dim, parts):
        steps = jax.random.uniform(jax.random.fold_in(jax.random.fold_in(key, 6), dim), (parts,), jnp.float32, low / len(pieces), largest / len(pieces))
        return jnp.repeat(jnp.exp(steps), dims[dim] // parts).reshape((-1,) + (1,) * (len(dims) - dim - 1))

    level = one(*pieces[0])
    for cut in pieces[1:]:
        level = level * one(*cut)
    return level


def different_ones(rng, rows, amount, top, lift):
    sequence = jax.random.permutation(jax.random.fold_in(rng, 1), amount)
    favour = sequence
    for power in range(3):
        favour = favour * favour // amount
    favour = favour * lift // amount
    tickets = jax.random.randint(jax.random.fold_in(rng, 2), (rows, amount), 0, 4096) + favour
    fixed_rows = jax.random.permutation(jax.random.fold_in(rng, 3), rows)[jnp.arange(amount) % rows]
    tickets = jnp.where(jnp.arange(rows)[:, None] == fixed_rows[None, :], 1 << 14, tickets)
    score = tickets * amount + jnp.arange(amount)
    return lax.top_k(score.astype(jnp.int32), top)[1].astype(jnp.int32)


def length_profile(amount, total, bound, skew):
    portions = [(1 << 20) // math.isqrt(rank ** skew) + 1 for rank in range(2, amount + 1)]
    surplus, given = total - bound - (amount - 1), [1] * (amount - 1)
    while surplus > 0:
        candidates = [i for i in range(amount - 1) if given[i] < bound]
        whole, left = sum([portions[i] for i in candidates]), surplus
        for i in candidates:
            addition = min(bound - given[i], max(1, left * portions[i] // whole), surplus)
            given[i] = given[i] + addition
            surplus = surplus - addition
    return np.array([bound] + given)


def ragged_sizes(own_key, count, total, reach, slope):
    if count == 2:
        one = jax.random.randint(own_key, (), max(1, total - reach), min(reach, total - 1) + 1)
        return jnp.stack([one, total - one])
    sizes = jnp.asarray(length_profile(count, total, reach, slope), jnp.int32)
    twos = (count - 1) // 2
    donor, taker = sizes[1:1 + 2 * twos:2], sizes[2:2 + 2 * twos:2]
    margin = jnp.minimum(donor - 1, reach - taker)
    moved = jax.random.randint(jax.random.fold_in(own_key, 1), (twos,), 0, 1 << 20) % (margin + 1)
    sizes = sizes.at[1:1 + 2 * twos:2].set(donor - moved).at[2:2 + 2 * twos:2].set(taker + moved)
    return sizes[jax.random.permutation(jax.random.fold_in(own_key, 2), count)]


def scatter_about(own_key, shape, scale, most, shards=(), held_as=jnp.bfloat16):
    level = block_levels(own_key, shape, shards, -0.22, 0.18) if shards else 1.0
    values = jax.random.normal(own_key, shape, jnp.float32) * scale * level
    return jnp.minimum(jnp.maximum(values, -most), most).astype(held_as)


def bell_draw_with(stream_key, dims, scale, limit, pieces, heavy, kind=jnp.bfloat16):
    values = scale * jax.random.normal(stream_key, dims, jnp.float32)
    if pieces:
        values = values * block_levels(stream_key, dims, pieces, -0.22, 0.18)
    return jnp.clip(spiked(values, jax.random.fold_in(stream_key, 3), *heavy), -limit, limit).astype(kind)


def setup_inputs(seed: int = 0) -> dict:
    streams_of = jax.random.split(jax.random.key(seed), 17)
    return {
        "attended": scatter_about(streams_of[0], (ROWS, D), 1.0, 6.0, ((0, 32),)),
        "residual": scatter_about(streams_of[1], (ROWS, D), 1.0, 6.0, ((0, 32),)),
        "new_kv": scatter_about(streams_of[2], (ROWS, KVW), 1.0, 6.0, ((0, 32),)),
        "kv_pool": scatter_about(streams_of[3], (POOL, PAGE, KVW), 1.0, 6.0, ((0, 32),)),
        "page_table": draw_page_table(jax.random.fold_in(streams_of[16], 71), 0),
        "out_weight": bell_draw_with(streams_of[5], (D, D), D ** -0.5, 0.3125, ((0, 32),), (0, 1, 32, 2.75)),
        "router": scatter_about(streams_of[6], (D, EXPERTS), D ** -0.5, 0.15625, ((0, 32),)),
        "attn_gain": jnp.clip(1.0 + 0.18 * jax.random.normal(streams_of[7], (D,), jnp.float32), 0.099609375, 1.8984375).astype(jnp.bfloat16),
        "ffn_gain": jnp.clip(1.0 + 0.18 * jax.random.normal(streams_of[8], (D,), jnp.float32), 0.099609375, 1.8984375).astype(jnp.bfloat16),
        "routes": different_ones(streams_of[9], ROWS, EXPERTS, TOP, 3276),
        "replica_pick": touch_ends(jax.random.randint(streams_of[10], (ROWS, TOP), 0, 5040), jax.random.fold_in(streams_of[10], 1), 0, 5039).astype(jnp.int32),
        "lengths": ragged_sizes(streams_of[11], 5, ROWS, ROWS // 2, 2).astype(jnp.int32),
        "slot_expert": draw_slot_expert(jax.random.fold_in(streams_of[16], 71), 0),
        "slot_capacity": draw_slot_capacity(jax.random.fold_in(streams_of[16], 71), 0),
        "slot_in": scatter_about(streams_of[14], (SLOTS, D, 2 * FFE), D ** -0.5, 0.15625, ((0, 8), (1, 4))),
        "slot_out": scatter_about(streams_of[15], (SLOTS, D, FFE), FFE ** -0.5, 0.25, ((0, 8), (1, 4))),
    }


eps_norm = 1e-06

def rms_scale(values, gain):
    mean_sq = lax.optimization_barrier(jnp.mean(values * values, axis=-1, keepdims=True))
    return values * lax.rsqrt(mean_sq + eps_norm) * gain.astype(jnp.float32)

def reference(attended, residual, new_kv, kv_pool, page_table, out_weight, router, attn_gain, ffn_gain, routes, replica_pick, lengths, slot_expert, slot_capacity, slot_in, slot_out):
    proj = jnp.dot(attended, out_weight, preferred_element_type=jnp.float32)
    hidden = (residual.astype(jnp.float32) + proj).astype(jnp.bfloat16)
    normed = rms_scale(hidden.astype(jnp.float32), attn_gain).astype(jnp.bfloat16)
    owner_page = jnp.arange(PAGES, dtype=jnp.int32) // PAGES_DEV
    dest_page = (owner_page * POOL_DEV + page_table).astype(jnp.int32)
    pool_out = kv_pool.at[dest_page].set(new_kv.reshape(PAGES, PAGE, KVW))
    logits = jnp.dot(normed, router, preferred_element_type=jnp.float32)
    picked = jnp.take_along_axis(logits, routes, axis=1)
    raised = jnp.exp(picked)
    gates = raised / lax.optimization_barrier(jnp.sum(raised, axis=1, keepdims=True))
    held = (slot_expert[None, :] == jnp.arange(EXPERTS, dtype=jnp.int32)[:, None]).astype(jnp.int32)
    copies = lax.optimization_barrier(jnp.sum(held, axis=1))
    rank = lax.optimization_barrier(jnp.sum((jnp.cumsum(held, axis=1) - held) * held, axis=0))
    wanted = replica_pick % copies[routes]
    matched = (slot_expert[None, None, :] == routes[:, :, None]) & (rank[None, None, :] == wanted[:, :, None])
    slot_ids = jnp.arange(SLOTS, dtype=jnp.int32)
    target = lax.optimization_barrier(jnp.sum(jnp.where(matched, slot_ids[None, None, :], 0), axis=2)).astype(jnp.int32)
    live = jnp.arange(ROWS, dtype=jnp.int32) < jnp.sum(lengths[:-1])
    w_in = slot_in.astype(jnp.float32)
    w_out = slot_out.astype(jnp.float32)

    def one_block(block):
        normed_b, target_b, live_b, gates_b = block
        flat_target = target_b.reshape(-1)
        flat_live = jnp.repeat(live_b, TOP)
        slot_hot = ((flat_target[:, None] == slot_ids[None, :]) & flat_live[:, None]).astype(jnp.int32)
        before = jnp.cumsum(slot_hot, axis=0) - slot_hot
        position = lax.optimization_barrier(jnp.sum(before * slot_hot, axis=1))
        kept = flat_live & (position < slot_capacity[flat_target])
        place = jnp.where(kept, flat_target * CAP + position, SLOTS * CAP).astype(jnp.int32)
        send = jnp.zeros((SLOTS * CAP, D), jnp.bfloat16).at[place].set(jnp.repeat(normed_b, TOP, axis=0), mode='drop')
        arrived = send.reshape(SLOTS, CAP, D).astype(jnp.float32)
        both = jnp.einsum('scd,sdf->scf', arrived, w_in)
        inner = (jax.nn.silu(both[..., :FFE]) * both[..., FFE:]).astype(jnp.bfloat16)
        inner = lax.optimization_barrier(inner).astype(jnp.float32)
        result = jnp.einsum('scf,sdf->scd', inner, w_out).astype(jnp.bfloat16)
        fetched = result.reshape(SLOTS * CAP, D)[jnp.minimum(place, SLOTS * CAP - 1)].astype(jnp.float32)
        weighted = jnp.where(kept[:, None], fetched, 0.0) * gates_b.reshape(-1)[:, None]
        return lax.optimization_barrier(jnp.sum(weighted.reshape(ROWS_DEV, TOP, D), axis=1))
    mixed = lax.map(one_block, (normed.reshape(DEVICES, ROWS_DEV, D), target.reshape(DEVICES, ROWS_DEV, TOP), live.reshape(DEVICES, ROWS_DEV), gates.reshape(DEVICES, ROWS_DEV, TOP))).reshape(ROWS, D)
    total = hidden.astype(jnp.float32) + mixed
    residual_out = total.astype(jnp.bfloat16)
    next_normed = rms_scale(total, ffn_gain).astype(jnp.bfloat16)
    return (residual_out, next_normed, pool_out)
```

```python
import jax
import jax.numpy as jnp
from jax import lax
from jax.sharding import PartitionSpec as P

eps_norm = 1e-06


def rms_scale(values, gain):
    mean_sq = jnp.mean(values * values, axis=-1, keepdims=True)
    return values * lax.rsqrt(mean_sq + eps_norm) * gain.astype(jnp.float32)


def on_device(
    attended,
    residual,
    new_kv,
    kv_pool,
    page_table,
    out_weight,
    router,
    attn_gain,
    ffn_gain,
    routes,
    replica_pick,
    lengths,
    slot_expert,
    slot_capacity,
    slot_in,
    slot_out,
):
    rows_dev, row_width = attended.shape
    experts_all = router.shape[1]
    slots_all = slot_expert.shape[0]
    top_count = routes.shape[1]
    holders = lax.axis_size("expert")
    slots_dev = slots_all // holders
    hidden_units = slot_out.shape[2]
    capacity = (rows_dev * top_count * 5 // (4 * slots_all) + 7) // 8 * 8
    bits = [1 << level for level in range(holders.bit_length() - 1)]

    side = -(-(experts_all + 2) // 128) * 128
    packed = jnp.concatenate(
        [
            out_weight,
            router,
            attn_gain[:, None],
            ffn_gain[:, None],
            jnp.zeros((out_weight.shape[0], side - experts_all - 2), jnp.bfloat16),
        ],
        axis=1,
    )
    packed_full = lax.all_gather(packed, ("dp", "expert"), axis=0, tiled=True)
    w_in = lax.all_gather(slot_in, "dp", axis=1, tiled=True)
    w_out = lax.all_gather(slot_out, "dp", axis=1, tiled=True)

    page_rows = kv_pool.shape[1]
    new_pages = new_kv.reshape(rows_dev // page_rows, page_rows, new_kv.shape[1])
    page_iota = lax.broadcasted_iota(jnp.int32, (kv_pool.shape[0], 1, 1), 0)
    pool_out = kv_pool
    for page in range(rows_dev // page_rows):
        pool_out = jnp.where(page_iota == page_table[page], new_pages[page][None], pool_out)

    same = slot_expert[:, None] == slot_expert[None, :]
    slot_before = (
        lax.broadcasted_iota(jnp.int32, (slots_all, slots_all), 0)
        < lax.broadcasted_iota(jnp.int32, (slots_all, slots_all), 1)
    )
    slot_copies = jnp.sum(same.astype(jnp.int32), axis=0)
    rank = jnp.sum((same & slot_before).astype(jnp.int32), axis=0)
    live_end = jnp.sum(lengths[:-1])
    row_first = lax.axis_index(("dp", "expert")) * rows_dev
    row_ids = row_first + lax.broadcasted_iota(jnp.int32, (rows_dev, 1), 0)
    live = row_ids < live_end
    chosen = jnp.zeros((rows_dev, slots_all), jnp.bool_)
    routed = jnp.zeros((rows_dev, experts_all), jnp.bool_)
    expert_iota = lax.broadcasted_iota(jnp.int32, (1, experts_all), 1)
    for k in range(top_count):
        route, pick = routes[:, k : k + 1], replica_pick[:, k : k + 1]
        chosen |= (route == slot_expert[None, :]) & (pick % slot_copies[None, :] == rank[None, :])
        routed |= route == expert_iota
    chosen &= live
    earlier = (
        lax.broadcasted_iota(jnp.int32, (rows_dev, rows_dev), 1)
        < lax.broadcasted_iota(jnp.int32, (rows_dev, rows_dev), 0)
    ).astype(jnp.bfloat16)
    position = jnp.dot(
        earlier, chosen.astype(jnp.bfloat16), preferred_element_type=jnp.float32
    )
    kept = chosen & (position < slot_capacity[None, :].astype(jnp.float32))
    place = jnp.where(kept, position, -1.0).astype(jnp.bfloat16)

    proj = jnp.dot(
        attended, packed_full[:, :row_width], preferred_element_type=jnp.float32
    )
    gain_first = packed_full[:, row_width + experts_all]
    gain_second = packed_full[:, row_width + experts_all + 1]
    router_full = packed_full[:, row_width : row_width + experts_all]
    hidden = (residual.astype(jnp.float32) + proj).astype(jnp.bfloat16)
    normed = rms_scale(hidden.astype(jnp.float32), gain_first).astype(jnp.bfloat16)
    logits = jnp.dot(normed, router_full, preferred_element_type=jnp.float32)
    raised = jnp.where(routed, jnp.exp(logits), 0.0)
    gates = raised / jnp.sum(raised, axis=1, keepdims=True)
    spread = (
        slot_expert[None, :] == lax.broadcasted_iota(jnp.int32, (experts_all, 1), 0)
    ).astype(jnp.float32)
    gate = jnp.where(kept, jnp.dot(gates, spread, precision=lax.Precision.HIGHEST), 0.0)
    gate_high = lax.reduce_precision(gate, 8, 7)
    gate_low = gate - gate_high

    meta = -(-3 * slots_all // 128) * 128
    table = jnp.concatenate(
        [
            place,
            gate_high.astype(jnp.bfloat16),
            gate_low.astype(jnp.bfloat16),
            jnp.zeros((rows_dev, meta - 3 * slots_all), jnp.bfloat16),
        ],
        axis=1,
    )
    blocks = {0: jnp.concatenate([normed, table], axis=1)}
    for bit in reversed(bits):
        pairs = [(i, i ^ bit) for i in range(holders)]
        for key in sorted(blocks):
            blocks[key ^ bit] = lax.ppermute(blocks[key], "expert", pairs)
    arrived = jnp.stack([blocks[key] for key in range(holders)])

    me = lax.axis_index("expert")
    tables = arrived[:, :, row_width : row_width + 3 * slots_all].reshape(
        holders, rows_dev, 3, slots_all
    )
    mine = lax.dynamic_slice_in_dim(tables, me * slots_dev, slots_dev, axis=3)
    mine = jnp.transpose(mine, (2, 0, 3, 1)).astype(jnp.float32)
    gate_rows = mine[1] + mine[2]
    spots = lax.broadcasted_iota(jnp.int32, (1, 1, capacity, 1), 2).astype(jnp.float32)
    hot = mine[0][:, :, None, :] == spots
    hot_low = hot.astype(jnp.bfloat16)
    slot_gate = jnp.sum(jnp.where(hot, gate_rows[:, :, None, :], 0.0), axis=3)

    rows_in = jnp.einsum(
        "hscr,hrd->hscd", hot_low, arrived[:, :, :row_width], preferred_element_type=jnp.float32
    ).astype(jnp.bfloat16)
    both = jnp.einsum("hscd,sdf->hscf", rows_in, w_in, preferred_element_type=jnp.float32)
    inner = (jax.nn.silu(both[..., :hidden_units]) * both[..., hidden_units:]).astype(jnp.bfloat16)
    result = jnp.einsum("hscf,sdf->hscd", inner, w_out, preferred_element_type=jnp.float32)
    scaled = (result * slot_gate[..., None]).astype(jnp.bfloat16)
    partial = jnp.einsum(
        "hscr,hscd->hrd", hot_low, scaled, preferred_element_type=jnp.float32
    ).astype(jnp.bfloat16)

    sums = {key: partial[key] for key in range(holders)}
    for bit in bits:
        pairs = [(i, i ^ bit) for i in range(holders)]
        for key in sorted(sums):
            if key & bit:
                came = lax.ppermute(sums.pop(key), "expert", pairs)
                joined = sums[key ^ bit].astype(jnp.float32) + came.astype(jnp.float32)
                last = bit == bits[-1]
                sums[key ^ bit] = joined if last else joined.astype(jnp.bfloat16)
    mixed = sums[0].astype(jnp.float32)
    total = hidden.astype(jnp.float32) + mixed
    residual_out = total.astype(jnp.bfloat16)
    next_normed = rms_scale(total, gain_second).astype(jnp.bfloat16)
    return (residual_out, next_normed, pool_out)


def solution(mesh):
    in_specs = (
        P(("dp", "expert"), None),
        P(("dp", "expert"), None),
        P(("dp", "expert"), None),
        P(("dp", "expert"), None, None),
        P(("dp", "expert")),
        P(("dp", "expert"), None),
        P(("dp", "expert"), None),
        P(("dp", "expert")),
        P(("dp", "expert")),
        P(("dp", "expert"), None),
        P(("dp", "expert"), None),
        P(),
        P(),
        P(),
        P("expert", "dp", None),
        P("expert", "dp", None),
    )
    out_specs = (
        P(("dp", "expert"), None),
        P(("dp", "expert"), None),
        P(("dp", "expert"), None, None),
    )
    return jax.shard_map(
        on_device, mesh=mesh, in_specs=in_specs, out_specs=out_specs, check_vma=False
    )
```

```python
import jax
import jax.numpy as jnp
from jax import lax
from jax.sharding import PartitionSpec as P

eps_norm = 1e-06


def rms_scale(values, gain):
    mean_sq = jnp.mean(values * values, axis=-1, keepdims=True)
    return values * lax.rsqrt(mean_sq + eps_norm) * gain.astype(jnp.float32)


def spread_by_doubling(block, bits):
    dp_bits = [1 << level for level in range(lax.axis_size("dp").bit_length() - 1)]
    outer = len(dp_bits) - 1 if dp_bits else 0
    steps = [("dp", bit, at) for at, bit in enumerate(reversed(dp_bits[1:]))]
    steps += [("expert", bit, outer + at) for at, bit in enumerate(reversed(bits))]
    steps += [("dp", bit, outer) for bit in dp_bits[:1]]
    held = block
    for name, bit, at in steps:
        pairs = [(i, i ^ bit) for i in range(lax.axis_size(name))]
        came = lax.ppermute(held, name, pairs)
        upper = (lax.axis_index(name) & bit) != 0
        held = jnp.stack([jnp.where(upper, came, held), jnp.where(upper, held, came)], axis=at)
    return held.reshape(-1, block.shape[1])


def halve_sums(sums, bit):
    pairs = [(i, i ^ bit) for i in range(lax.axis_size("expert"))]
    kept_sums = {}
    for key in sorted(sums):
        if key & bit:
            came = lax.ppermute(sums[key], "expert", pairs)
            joined = sums[key ^ bit].astype(jnp.float32) + came.astype(jnp.float32)
            last = len(sums) == 2
            kept_sums[key ^ bit] = joined if last else joined.astype(jnp.bfloat16)
    return kept_sums


def on_device(
    attended,
    residual,
    new_kv,
    kv_pool,
    page_table,
    out_weight,
    router,
    attn_gain,
    ffn_gain,
    routes,
    replica_pick,
    lengths,
    slot_expert,
    slot_capacity,
    slot_in,
    slot_out,
):
    rows_dev, row_width = attended.shape
    experts_all = router.shape[1]
    slots_all = slot_expert.shape[0]
    top_count = routes.shape[1]
    holders = lax.axis_size("expert")
    slots_dev = slots_all // holders
    hidden_units = slot_out.shape[2]
    capacity = (rows_dev * top_count * 5 // (4 * slots_all) + 7) // 8 * 8
    bits = [1 << level for level in range(holders.bit_length() - 1)]

    side = -(-(experts_all + 2) // 128) * 128
    packed = jnp.concatenate(
        [
            out_weight,
            router,
            attn_gain[:, None],
            ffn_gain[:, None],
            jnp.zeros((out_weight.shape[0], side - experts_all - 2), jnp.bfloat16),
        ],
        axis=1,
    )
    packed_full = spread_by_doubling(packed, bits)
    w_in = lax.all_gather(slot_in, "dp", axis=1, tiled=True)
    features = slot_out.shape[1]
    first = min(features, -(-features // 256) * 128)
    cuts = [(0, first), (first, features)] if first < features else [(0, features)]
    w_out = [lax.all_gather(slot_out[:, lo:hi], "dp", axis=1, tiled=True) for lo, hi in cuts]

    page_rows = kv_pool.shape[1]
    new_pages = new_kv.reshape(rows_dev // page_rows, page_rows, new_kv.shape[1])
    page_iota = lax.broadcasted_iota(jnp.int32, (kv_pool.shape[0], 1, 1), 0)
    pool_out = kv_pool
    for page in range(rows_dev // page_rows):
        pool_out = jnp.where(page_iota == page_table[page], new_pages[page][None], pool_out)

    same = slot_expert[:, None] == slot_expert[None, :]
    slot_before = (
        lax.broadcasted_iota(jnp.int32, (slots_all, slots_all), 0)
        < lax.broadcasted_iota(jnp.int32, (slots_all, slots_all), 1)
    )
    slot_copies = jnp.sum(same.astype(jnp.int32), axis=0)
    rank = jnp.sum((same & slot_before).astype(jnp.int32), axis=0)
    live_end = jnp.sum(lengths[:-1])
    row_first = lax.axis_index(("dp", "expert")) * rows_dev
    row_ids = row_first + lax.broadcasted_iota(jnp.int32, (rows_dev, 1), 0)
    live = row_ids < live_end
    chosen = jnp.zeros((rows_dev, slots_all), jnp.bool_)
    routed = jnp.zeros((rows_dev, experts_all), jnp.bool_)
    expert_iota = lax.broadcasted_iota(jnp.int32, (1, experts_all), 1)
    for k in range(top_count):
        route, pick = routes[:, k : k + 1], replica_pick[:, k : k + 1]
        chosen |= (route == slot_expert[None, :]) & (pick % slot_copies[None, :] == rank[None, :])
        routed |= route == expert_iota
    chosen &= live
    earlier = (
        lax.broadcasted_iota(jnp.int32, (rows_dev, rows_dev), 1)
        < lax.broadcasted_iota(jnp.int32, (rows_dev, rows_dev), 0)
    ).astype(jnp.bfloat16)
    position = jnp.dot(
        earlier, chosen.astype(jnp.bfloat16), preferred_element_type=jnp.float32
    )
    kept = chosen & (position < slot_capacity[None, :].astype(jnp.float32))
    place = jnp.where(kept, position, -1.0).astype(jnp.bfloat16)

    proj = jnp.dot(
        attended, packed_full[:, :row_width], preferred_element_type=jnp.float32
    )
    gain_first = packed_full[:, row_width + experts_all]
    gain_second = packed_full[:, row_width + experts_all + 1]
    router_full = packed_full[:, row_width : row_width + experts_all]
    hidden = (residual.astype(jnp.float32) + proj).astype(jnp.bfloat16)
    normed = rms_scale(hidden.astype(jnp.float32), gain_first).astype(jnp.bfloat16)
    logits = jnp.dot(normed, router_full, preferred_element_type=jnp.float32)
    raised = jnp.where(routed, jnp.exp(logits), 0.0)
    gates = raised / jnp.sum(raised, axis=1, keepdims=True)
    spread = (
        slot_expert[None, :] == lax.broadcasted_iota(jnp.int32, (experts_all, 1), 0)
    ).astype(jnp.float32)
    gate = jnp.where(kept, jnp.dot(gates, spread, precision=lax.Precision.HIGHEST), 0.0)
    gate_high = lax.reduce_precision(gate, 8, 7)
    gate_low = gate - gate_high

    meta = -(-3 * slots_all // 128) * 128
    table = jnp.concatenate(
        [
            place,
            gate_high.astype(jnp.bfloat16),
            gate_low.astype(jnp.bfloat16),
            jnp.zeros((rows_dev, meta - 3 * slots_all), jnp.bfloat16),
        ],
        axis=1,
    )
    blocks = {0: jnp.concatenate([normed, table], axis=1)}
    for bit in reversed(bits):
        pairs = [(i, i ^ bit) for i in range(holders)]
        for key in sorted(blocks):
            blocks[key ^ bit] = lax.ppermute(blocks[key], "expert", pairs)
    arrived = jnp.stack([blocks[key] for key in range(holders)])

    me = lax.axis_index("expert")
    tables = arrived[:, :, row_width : row_width + 3 * slots_all].reshape(
        holders, rows_dev, 3, slots_all
    )
    mine = lax.dynamic_slice_in_dim(tables, me * slots_dev, slots_dev, axis=3)
    mine = jnp.transpose(mine, (2, 0, 3, 1)).astype(jnp.float32)
    gate_rows = mine[1] + mine[2]
    spots = lax.broadcasted_iota(jnp.int32, (1, 1, capacity, 1), 2).astype(jnp.float32)
    hot = mine[0][:, :, None, :] == spots
    hot_low = hot.astype(jnp.bfloat16)
    slot_gate = jnp.sum(jnp.where(hot, gate_rows[:, :, None, :], 0.0), axis=3)

    rows_in = jnp.einsum(
        "hscr,hrd->hscd", hot_low, arrived[:, :, :row_width], preferred_element_type=jnp.float32
    ).astype(jnp.bfloat16)
    both = jnp.einsum("hscd,sdf->hscf", rows_in, w_in, preferred_element_type=jnp.float32)
    inner = (jax.nn.silu(both[..., :hidden_units]) * both[..., hidden_units:]).astype(jnp.bfloat16)
    trees = []
    for part in w_out:
        if trees and bits:
            part = lax.optimization_barrier((trees[-1], part))[1]
        result = jnp.einsum("hscf,sdf->hscd", inner, part, preferred_element_type=jnp.float32)
        scaled = (result * slot_gate[..., None]).astype(jnp.bfloat16)
        partial = jnp.einsum(
            "hscr,hscd->hrd", hot_low, scaled, preferred_element_type=jnp.float32
        ).astype(jnp.bfloat16)
        sums = {key: partial[key] for key in range(holders)}
        trees.append(halve_sums(sums, bits[0]) if bits else sums)
    pieces = []
    for sums in trees:
        for bit in bits[1:]:
            sums = halve_sums(sums, bit)
        pieces.append(sums[0].astype(jnp.float32).reshape(rows_dev, lax.axis_size("dp"), -1))
    mixed = jnp.concatenate(pieces, axis=2).reshape(rows_dev, row_width)
    total = hidden.astype(jnp.float32) + mixed
    residual_out = total.astype(jnp.bfloat16)
    next_normed = rms_scale(total, gain_second).astype(jnp.bfloat16)
    return (residual_out, next_normed, pool_out)


def solution(mesh):
    in_specs = (
        P(("dp", "expert"), None),
        P(("dp", "expert"), None),
        P(("dp", "expert"), None),
        P(("dp", "expert"), None, None),
        P(("dp", "expert")),
        P(("dp", "expert"), None),
        P(("dp", "expert"), None),
        P(("dp", "expert")),
        P(("dp", "expert")),
        P(("dp", "expert"), None),
        P(("dp", "expert"), None),
        P(),
        P(),
        P(),
        P("expert", "dp", None),
        P("expert", "dp", None),
    )
    out_specs = (
        P(("dp", "expert"), None),
        P(("dp", "expert"), None),
        P(("dp", "expert"), None, None),
    )
    return jax.shard_map(
        on_device, mesh=mesh, in_specs=in_specs, out_specs=out_specs, check_vma=False
    )
```

```python
import jax
import jax.numpy as jnp
from jax import lax
from jax.sharding import PartitionSpec as P

eps_norm = 1e-06


def rms_scale(values, gain):
    mean_sq = jnp.mean(values * values, axis=-1, keepdims=True)
    return values * lax.rsqrt(mean_sq + eps_norm) * gain.astype(jnp.float32)


def spread_by_doubling(block, bits, low_first):
    dp_bits = [1 << level for level in range(lax.axis_size("dp").bit_length() - 1)]
    outer = len(dp_bits) - 1 if dp_bits else 0
    steps = [("dp", bit, at) for at, bit in enumerate(reversed(dp_bits[1:]))]
    expert_steps = [("expert", bit, outer + at) for at, bit in enumerate(reversed(bits))]
    if low_first and bits:
        expert_steps = [("expert", bits[0], outer)] + expert_steps[:-1]
    steps += expert_steps
    steps += [("dp", bit, outer) for bit in dp_bits[:1]]
    held = block
    for name, bit, at in steps:
        pairs = [(i, i ^ bit) for i in range(lax.axis_size(name))]
        came = lax.ppermute(held, name, pairs)
        upper = (lax.axis_index(name) & bit) != 0
        held = jnp.stack([jnp.where(upper, came, held), jnp.where(upper, held, came)], axis=at)
    return held.reshape(-1, block.shape[1])


def halve_sums(sums, bit):
    pairs = [(i, i ^ bit) for i in range(lax.axis_size("expert"))]
    kept_sums = {}
    for key in sorted(sums):
        if key & bit:
            came = lax.ppermute(sums[key], "expert", pairs)
            joined = sums[key ^ bit].astype(jnp.float32) + came.astype(jnp.float32)
            last = len(sums) == 2
            kept_sums[key ^ bit] = joined if last else joined.astype(jnp.bfloat16)
    return kept_sums


def on_device(
    attended,
    residual,
    new_kv,
    kv_pool,
    page_table,
    out_weight,
    router,
    attn_gain,
    ffn_gain,
    routes,
    replica_pick,
    lengths,
    slot_expert,
    slot_capacity,
    slot_in,
    slot_out,
):
    rows_dev, row_width = attended.shape
    experts_all = router.shape[1]
    slots_all = slot_expert.shape[0]
    top_count = routes.shape[1]
    holders = lax.axis_size("expert")
    slots_dev = slots_all // holders
    hidden_units = slot_out.shape[2]
    capacity = (rows_dev * top_count * 5 // (4 * slots_all) + 7) // 8 * 8
    bits = [1 << level for level in range(holders.bit_length() - 1)]

    side = -(-(experts_all + 2) // 128) * 128
    packed = jnp.concatenate(
        [
            out_weight[:, row_width // 2 :],
            router,
            attn_gain[:, None],
            ffn_gain[:, None],
            jnp.zeros((out_weight.shape[0], side - experts_all - 2), jnp.bfloat16),
        ],
        axis=1,
    )
    half = row_width // 2
    left_full = spread_by_doubling(out_weight[:, :half], bits, False)
    right_full = spread_by_doubling(packed, bits, True)
    w_in = lax.all_gather(slot_in, "dp", axis=1, tiled=True)
    features = slot_out.shape[1]
    cuts = [(lo, min(lo + 128, features)) for lo in range(0, features, 128)]
    w_out = [lax.all_gather(slot_out[:, lo:hi], "dp", axis=1, tiled=True) for lo, hi in cuts]

    page_rows = kv_pool.shape[1]
    new_pages = new_kv.reshape(rows_dev // page_rows, page_rows, new_kv.shape[1])
    page_iota = lax.broadcasted_iota(jnp.int32, (kv_pool.shape[0], 1, 1), 0)
    pool_out = kv_pool
    for page in range(rows_dev // page_rows):
        pool_out = jnp.where(page_iota == page_table[page], new_pages[page][None], pool_out)

    same = slot_expert[:, None] == slot_expert[None, :]
    slot_before = (
        lax.broadcasted_iota(jnp.int32, (slots_all, slots_all), 0)
        < lax.broadcasted_iota(jnp.int32, (slots_all, slots_all), 1)
    )
    slot_copies = jnp.sum(same.astype(jnp.int32), axis=0)
    rank = jnp.sum((same & slot_before).astype(jnp.int32), axis=0)
    live_end = jnp.sum(lengths[:-1])
    row_first = lax.axis_index(("dp", "expert")) * rows_dev
    row_ids = row_first + lax.broadcasted_iota(jnp.int32, (rows_dev, 1), 0)
    live = row_ids < live_end
    chosen = jnp.zeros((rows_dev, slots_all), jnp.bool_)
    routed = jnp.zeros((rows_dev, experts_all), jnp.bool_)
    expert_iota = lax.broadcasted_iota(jnp.int32, (1, experts_all), 1)
    for k in range(top_count):
        route, pick = routes[:, k : k + 1], replica_pick[:, k : k + 1]
        chosen |= (route == slot_expert[None, :]) & (pick % slot_copies[None, :] == rank[None, :])
        routed |= route == expert_iota
    chosen &= live
    earlier = (
        lax.broadcasted_iota(jnp.int32, (rows_dev, rows_dev), 1)
        < lax.broadcasted_iota(jnp.int32, (rows_dev, rows_dev), 0)
    ).astype(jnp.bfloat16)
    position = jnp.dot(
        earlier, chosen.astype(jnp.bfloat16), preferred_element_type=jnp.float32
    )
    kept = chosen & (position < slot_capacity[None, :].astype(jnp.float32))
    place = jnp.where(kept, position, -1.0).astype(jnp.bfloat16)

    rest = row_width - half
    proj = jnp.concatenate(
        [
            jnp.dot(attended, left_full, preferred_element_type=jnp.float32),
            jnp.dot(attended, right_full[:, :rest], preferred_element_type=jnp.float32),
        ],
        axis=1,
    )
    gain_first = right_full[:, rest + experts_all]
    gain_second = right_full[:, rest + experts_all + 1]
    router_full = right_full[:, rest : rest + experts_all]
    hidden = (residual.astype(jnp.float32) + proj).astype(jnp.bfloat16)
    normed = rms_scale(hidden.astype(jnp.float32), gain_first).astype(jnp.bfloat16)
    logits = jnp.dot(normed, router_full, preferred_element_type=jnp.float32)
    raised = jnp.where(routed, jnp.exp(logits), 0.0)
    gates = raised / jnp.sum(raised, axis=1, keepdims=True)
    spread = (
        slot_expert[None, :] == lax.broadcasted_iota(jnp.int32, (experts_all, 1), 0)
    ).astype(jnp.float32)
    gate = jnp.where(kept, jnp.dot(gates, spread, precision=lax.Precision.HIGHEST), 0.0)
    gate_high = lax.reduce_precision(gate, 8, 7)
    gate_low = gate - gate_high

    meta = -(-3 * slots_all // 128) * 128
    table = jnp.concatenate(
        [
            place,
            gate_high.astype(jnp.bfloat16),
            gate_low.astype(jnp.bfloat16),
            jnp.zeros((rows_dev, meta - 3 * slots_all), jnp.bfloat16),
        ],
        axis=1,
    )
    blocks = {0: jnp.concatenate([normed, table], axis=1)}
    for bit in reversed(bits):
        pairs = [(i, i ^ bit) for i in range(holders)]
        for key in sorted(blocks):
            blocks[key ^ bit] = lax.ppermute(blocks[key], "expert", pairs)
    arrived = jnp.stack([blocks[key] for key in range(holders)])

    me = lax.axis_index("expert")
    tables = arrived[:, :, row_width : row_width + 3 * slots_all].reshape(
        holders, rows_dev, 3, slots_all
    )
    mine = lax.dynamic_slice_in_dim(tables, me * slots_dev, slots_dev, axis=3)
    mine = jnp.transpose(mine, (2, 0, 3, 1)).astype(jnp.float32)
    gate_rows = mine[1] + mine[2]
    spots = lax.broadcasted_iota(jnp.int32, (1, 1, capacity, 1), 2).astype(jnp.float32)
    hot = mine[0][:, :, None, :] == spots
    hot_low = hot.astype(jnp.bfloat16)
    slot_gate = jnp.sum(jnp.where(hot, gate_rows[:, :, None, :], 0.0), axis=3)

    rows_in = jnp.einsum(
        "hscr,hrd->hscd", hot_low, arrived[:, :, :row_width], preferred_element_type=jnp.float32
    ).astype(jnp.bfloat16)
    both = jnp.einsum("hscd,sdf->hscf", rows_in, w_in, preferred_element_type=jnp.float32)
    inner = (jax.nn.silu(both[..., :hidden_units]) * both[..., hidden_units:]).astype(jnp.bfloat16)
    trees = []
    for part in w_out:
        if trees and bits:
            part = lax.optimization_barrier((trees[-1], part))[1]
        result = jnp.einsum("hscf,sdf->hscd", inner, part, preferred_element_type=jnp.float32)
        scaled = (result * slot_gate[..., None]).astype(jnp.bfloat16)
        partial = jnp.einsum(
            "hscr,hscd->hrd", hot_low, scaled, preferred_element_type=jnp.float32
        ).astype(jnp.bfloat16)
        sums = {key: partial[key] for key in range(holders)}
        trees.append(halve_sums(sums, bits[0]) if bits else sums)
    pieces = []
    for sums in trees:
        for bit in bits[1:]:
            sums = halve_sums(sums, bit)
        pieces.append(sums[0].astype(jnp.float32).reshape(rows_dev, lax.axis_size("dp"), -1))
    mixed = jnp.concatenate(pieces, axis=2).reshape(rows_dev, row_width)
    total = hidden.astype(jnp.float32) + mixed
    residual_out = total.astype(jnp.bfloat16)
    next_normed = rms_scale(total, gain_second).astype(jnp.bfloat16)
    return (residual_out, next_normed, pool_out)


def solution(mesh):
    in_specs = (
        P(("dp", "expert"), None),
        P(("dp", "expert"), None),
        P(("dp", "expert"), None),
        P(("dp", "expert"), None, None),
        P(("dp", "expert")),
        P(("dp", "expert"), None),
        P(("dp", "expert"), None),
        P(("dp", "expert")),
        P(("dp", "expert")),
        P(("dp", "expert"), None),
        P(("dp", "expert"), None),
        P(),
        P(),
        P(),
        P("expert", "dp", None),
        P("expert", "dp", None),
    )
    out_specs = (
        P(("dp", "expert"), None),
        P(("dp", "expert"), None),
        P(("dp", "expert"), None, None),
    )
    return jax.shard_map(
        on_device, mesh=mesh, in_specs=in_specs, out_specs=out_specs, check_vma=False
    )
```
